32 devices in a mesh: dom: 8 (over y, x, core), grp: 4 (over z).
Axes of the slice: x: 2, y: 2, z: 4, core: 2. Of those that a mesh axis runs over, the one named last changes fastest.
Arguments:
- features: bfloat16 [65536, 256], P(('dom', 'grp')), may hold values from -6 to 6
- edge_src: int32 [524288], P(('dom', 'grp')), may hold values from 0 to 2303, as said below
- edge_dst: int32 [524288], P(('dom', 'grp')), may hold values from 0 to 2047, as said below
- edge_count: int32 [32], P(('dom', 'grp')), may hold values from 4096 to 16384, as said below
- halo_index: int32 [32, 32, 8], P(('dom', 'grp')), may hold values from 0 to 2047
- request_rows: int32 [32, 32, 16], P(('dom', 'grp')), may hold values from 0 to 2047, as said below
- pair_ends: int32 [65536, 2], P(('dom', 'grp')), may hold values from 0 to 511
- labels: int32 [65536], P(('dom', 'grp')), may hold values 0 or 1
- pair_weight: float32 [65536], P(('dom', 'grp')), may hold values from 0.25 to 4
- w_self: bfloat16 [256, 256], replicated, may hold values from -0.375 to 0.375
- w_neigh: bfloat16 [256, 256], replicated, may hold values from -0.375 to 0.375
- w_hidden: bfloat16 [512, 256], replicated, may hold values from -0.25 to 0.25
- b_hidden: float32 [256], replicated, may hold values from -3 to 3
- w_out: float32 [256], replicated, may hold values from -0.375 to 0.375
Outputs:
- logits: float32 [65536], P(('dom', 'grp'))
- grad_features: float32 [65536, 256], P(('dom', 'grp'))
- grad_w_self: float32 [256, 256], replicated
- grad_w_neigh: float32 [256, 256], replicated
- grad_w_hidden: float32 [512, 256], replicated
- grad_b_hidden: float32 [256], replicated
- grad_w_out: float32 [256], replicated
The draws below stay inside these ranges and needn't reach their ends.
Inputs may be any that keep to these rules, and one draw needn't show every extreme that they name: `edge_src`: a row of the partition's own table. `edge_dst`: a local node of the partition; slots at or past edge_count are not live and hold arbitrary values. `edge_count`: some partition has exactly 16384 live slots. `halo_index`: local rows of the sending partition; 8 to every partition, itself included. `request_rows`: local rows of the owning partition, distinct and increasing within each list of 16. `pair_ends`: rows of the shard's own received rows.
All inputs are finite; a program needn't handle non-finite values. No bound on the sum of `labels` on one device may be relied on, other than what follows from the above.
Results may differ from the reference program's by a relative error of at most 0.02.
The reference program's roundings to bfloat16 on the way count: a program that leaves them out, or rounds other values in their place, can miss the bound.
Values may be sent and summed in bfloat16 or wider, within the bound.
A program may use at most 192 MiB of HBM per device.

```python
import math
import jax
import jax.numpy as jnp
from jax import lax

D = 256
NODE_DEV = 2048
HALO = 8
REQ = 16
TE_DEV = 2048
PARTITIONS = 32
EDGE_DEV = 16384
NODES = 65536
EDGES = 524288
TRAIN = 65536
RECEIVED = 512


def draw_edge_src(key, part):
    key_one, key_two, key_three = jax.random.split(key, 3)
    coin_flip = jax.random.randint(key_one, (EDGES,), 0, 2)
    local_rows = jax.random.randint(key_two, (EDGES,), 0, NODE_DEV)
    remote_rows = NODE_DEV + jax.random.randint(key_three, (EDGES,), 0, HALO * PARTITIONS)
    return jnp.where(coin_flip == 0, local_rows, remote_rows).astype(jnp.int32)


def draw_edge_dst(key, part):
    key_one, key_two = jax.random.split(key, 2)
    first_draw = jax.random.randint(key_one, (EDGES,), 0, NODE_DEV)
    second_draw = jax.random.randint(key_two, (EDGES,), 0, NODE_DEV)
    return (first_draw * second_draw // (NODE_DEV - 1)).astype(jnp.int32)


def draw_edge_count(key, part):
    key_one, key_two = jax.random.split(key, 2)
    divisor = 1 + jax.random.randint(key_one, (PARTITIONS,), 0, 4)
    counts = EDGE_DEV // divisor
    full_one = jax.random.randint(key_two, (), 0, PARTITIONS)
    return jnp.where(jnp.arange(PARTITIONS) == full_one, EDGE_DEV, counts).astype(jnp.int32)


def draw_request_rows(key, part):
    stride = NODE_DEV // REQ
    offsets = jax.random.randint(key, (PARTITIONS, PARTITIONS, REQ), 0, stride)
    return (jnp.arange(REQ, dtype=jnp.int32)[None, None, :] * stride + offsets).astype(jnp.int32)


def set_ends(entries, stream_key, smallest, top_value):
    shape = entries.shape
    spot = [jax.random.randint(jax.random.fold_in(stream_key, axis), (), 0, shape[axis]) for axis in range(len(shape))]
    entries = entries.at[tuple(spot)].set(smallest)
    longest = shape.index(max(shape))
    spot[longest] = (spot[longest] + 1) % shape[longest]
    return entries.at[tuple(spot)].set(top_value)


def levels(key, extent, cuts, smallest, top_value):
    level = 1.0
    for dim, shards_of in cuts:
        heights = jax.random.uniform(jax.random.fold_in(jax.random.fold_in(key, 6), dim), (shards_of,), jnp.float32, smallest / len(cuts), top_value / len(cuts))
        level = level * jnp.repeat(jnp.exp(heights), extent[dim] // shards_of).reshape((-1,) + (1,) * (len(extent) - 1 - dim))
    return level


def noise(own_key, extent, width, most, cuts=(), kind=jnp.bfloat16):
    level = levels(own_key, extent, cuts, -0.22, 0.18) if cuts else 1.0
    entries = jax.random.normal(own_key, extent, jnp.float32) * width * level
    return jnp.minimum(jnp.maximum(entries, -most), most).astype(kind)


def setup_inputs(seed: int = 0) -> dict:
    streams_of = jax.random.split(jax.random.key(seed), 15)
    features = noise(streams_of[0], (NODES, D), 1.0, 6.0, ((0, 32),))
    edge_src = draw_edge_src(jax.random.fold_in(streams_of[14], 71), 0)
    edge_dst = draw_edge_dst(jax.random.fold_in(streams_of[14], 71), 0)
    edge_count = draw_edge_count(jax.random.fold_in(streams_of[14], 71), 0)
    halo_index = set_ends(jax.random.randint(streams_of[4], (PARTITIONS, PARTITIONS, HALO), 0, NODE_DEV), jax.random.fold_in(streams_of[4], 1), 0, NODE_DEV - 1).astype(jnp.int32)
    request_rows = draw_request_rows(jax.random.fold_in(streams_of[14], 71), 0)
    pair_ends = set_ends(jax.random.randint(streams_of[6], (TRAIN, 2), 0, RECEIVED), jax.random.fold_in(streams_of[6], 1), 0, RECEIVED - 1).astype(jnp.int32)
    labels = set_ends((jax.random.randint(streams_of[7], (TRAIN,), 0, 2) < 1).astype(jnp.int32), jax.random.fold_in(streams_of[7], 1), 0, 1)
    pair_weight = jnp.clip(jnp.exp(math.log(4.0) - 2.7725887 * jax.random.uniform(streams_of[8], (TRAIN,), jnp.float32) ** levels(streams_of[8], (TRAIN,), ((0, 32),), -0.2, 0.2)), 0.25, 4.0)
    w_self = noise(streams_of[9], (D, D), D ** -0.5, 0.375)
    w_neigh = noise(streams_of[10], (D, D), D ** -0.5, 0.375)
    w_hidden = noise(streams_of[11], (2 * D, D), (2 * D) ** -0.5, 0.25)
    b_hidden = noise(streams_of[12], (D,), 0.5, 3.0, (), jnp.float32)
    w_out = noise(streams_of[13], (D,), D ** -0.5, 0.375, (), jnp.float32)
    return dict(features=features, edge_src=edge_src, edge_dst=edge_dst, edge_count=edge_count, halo_index=halo_index, request_rows=request_rows, pair_ends=pair_ends, labels=labels, pair_weight=pair_weight, w_self=w_self, w_neigh=w_neigh, w_hidden=w_hidden, b_hidden=b_hidden, w_out=w_out)


def encode_one(own_rows, halo_rows, src_slots, dst_slots, live_count, w_self, w_neigh):
    row_table = jnp.concatenate([own_rows, halo_rows], axis=0)
    slot_ids = jnp.arange(src_slots.shape[0], dtype=jnp.int32)
    alive_slot = slot_ids < live_count
    dst_index = jnp.where(alive_slot, dst_slots, NODE_DEV).astype(jnp.int32)
    gathered = row_table[src_slots].astype(jnp.float32)
    agg_sums = jax.ops.segment_sum(gathered, dst_index, num_segments=NODE_DEV + 1)[:NODE_DEV]
    degree = jax.ops.segment_sum(alive_slot.astype(jnp.float32), dst_index, num_segments=NODE_DEV + 1)[:NODE_DEV]
    aggregate = (agg_sums / jnp.maximum(degree, 1.0)[:, None]).astype(jnp.bfloat16)
    embedding = (jnp.dot(own_rows, w_self, preferred_element_type=jnp.float32)
                 + jnp.dot(aggregate, w_neigh, preferred_element_type=jnp.float32)).astype(jnp.bfloat16)
    return embedding, aggregate, degree


def reference(features, edge_src, edge_dst, edge_count, halo_index, request_rows, pair_ends, labels, pair_weight, w_self, w_neigh, w_hidden, b_hidden, w_out):
    part_count = PARTITIONS
    own_rows = features.reshape(part_count, NODE_DEV, D)
    senders = jnp.arange(part_count, dtype=jnp.int32)[:, None, None]
    sent_rows = own_rows[senders, halo_index]
    arriving = jnp.transpose(sent_rows, (1, 0, 2, 3)).reshape(part_count, part_count * HALO, D)
    src_slots = edge_src.reshape(part_count, EDGE_DEV)
    dst_slots = edge_dst.reshape(part_count, EDGE_DEV)

    def encode_step(packed):
        return encode_one(packed[0], packed[1], packed[2], packed[3], packed[4], w_self, w_neigh)

    embedding, aggregate, degree = lax.map(encode_step, (own_rows, arriving, src_slots, dst_slots, edge_count))

    end_pairs = pair_ends.reshape(part_count, TE_DEV, 2)
    flag_rows = labels.reshape(part_count, TE_DEV).astype(jnp.float32)
    weight_rows = pair_weight.reshape(part_count, TE_DEV)
    owners = jnp.arange(part_count, dtype=jnp.int32)[:, None]

    def decode_step(carry, packed):
        emb_grad, grad_hidden, grad_bias, grad_out = carry
        wanted_rows, pair_end, flag_row, weight_row = packed
        received = embedding[owners, wanted_rows].reshape(part_count * REQ, D)
        pair_input = jnp.concatenate([received[pair_end[:, 0]], received[pair_end[:, 1]]], axis=1)
        pre_act = jnp.dot(pair_input, w_hidden, preferred_element_type=jnp.float32) + b_hidden
        hidden = jnp.maximum(pre_act, 0.0)
        logits = jnp.dot(hidden, w_out, precision=lax.Precision.HIGHEST)
        slope_term = weight_row * (jax.nn.sigmoid(logits) - flag_row)
        grad_out = grad_out + jnp.dot(slope_term, hidden, precision=lax.Precision.HIGHEST)
        delta_act = jnp.where(pre_act > 0, slope_term[:, None] * w_out[None, :], 0.0)
        grad_bias = grad_bias + jnp.sum(delta_act, axis=0)
        delta_b = delta_act.astype(jnp.bfloat16)
        grad_hidden = grad_hidden + jnp.dot(pair_input.T, delta_b, preferred_element_type=jnp.float32)
        pair_grad = jnp.dot(delta_b, w_hidden.T, preferred_element_type=jnp.float32)
        received_grad = (jax.ops.segment_sum(pair_grad[:, :D], pair_end[:, 0], num_segments=part_count * REQ)
                         + jax.ops.segment_sum(pair_grad[:, D:], pair_end[:, 1], num_segments=part_count * REQ))
        received_grad_b = lax.optimization_barrier(received_grad.astype(jnp.bfloat16))
        emb_grad = emb_grad.at[owners, wanted_rows].add(received_grad_b.astype(jnp.float32).reshape(part_count, REQ, D))
        return (emb_grad, grad_hidden, grad_bias, grad_out), logits

    start = (jnp.zeros((part_count, NODE_DEV, D), jnp.float32), jnp.zeros((2 * D, D), jnp.float32),
             jnp.zeros((D,), jnp.float32), jnp.zeros((D,), jnp.float32))
    final, logit_rows = lax.scan(decode_step, start, (request_rows, end_pairs, flag_rows, weight_rows))
    emb_grad, grad_hidden, grad_bias, grad_out = final
    grad_b = emb_grad.astype(jnp.bfloat16)

    def encode_back(packed):
        own_part, agg_part, deg_part, grad_part, src_part, dst_part, count_part = packed
        grad_self = jnp.dot(own_part.T, grad_part, preferred_element_type=jnp.float32)
        grad_neigh = jnp.dot(agg_part.T, grad_part, preferred_element_type=jnp.float32)
        direct = jnp.dot(grad_part, w_self.T, preferred_element_type=jnp.float32)
        agg_grad = jnp.dot(grad_part, w_neigh.T, preferred_element_type=jnp.float32) / jnp.maximum(deg_part, 1.0)[:, None]
        padded = jnp.concatenate([agg_grad, jnp.zeros((1, D), jnp.float32)], axis=0)
        slot_ids = jnp.arange(src_part.shape[0], dtype=jnp.int32)
        dst_index = jnp.where(slot_ids < count_part, dst_part, NODE_DEV).astype(jnp.int32)
        table_grad = jax.ops.segment_sum(padded[dst_index], src_part, num_segments=NODE_DEV + part_count * HALO)
        return (direct + table_grad[:NODE_DEV], table_grad[NODE_DEV:].reshape(part_count, HALO, D), grad_self, grad_neigh)

    local_grad, halo_back, self_terms, neigh_terms = lax.map(
        encode_back, (own_rows, aggregate, degree, grad_b, src_slots, dst_slots, edge_count))
    returned = jnp.transpose(halo_back, (1, 0, 2, 3))
    local_grad = local_grad.at[senders, halo_index].add(returned)
    return (logit_rows.reshape(part_count * TE_DEV), local_grad.reshape(part_count * NODE_DEV, D),
            jnp.sum(self_terms, axis=0), jnp.sum(neigh_terms, axis=0), grad_hidden, grad_bias, grad_out)
```

```python
import functools

import jax
import jax.numpy as jnp
from jax import lax
from jax.experimental import pallas as pl
from jax.experimental.pallas import tpu as pltpu
from jax.sharding import PartitionSpec as P

F32 = jnp.float32
BF16 = jnp.bfloat16
VMEM_LIMIT = 60 * 1024 * 1024
NN = (((1,), (0,)), ((), ()))
NT = (((1,), (1,)), ((), ()))
TN = (((0,), (0,)), ((), ()))


def dot(left, right, dims=NN):
    return lax.dot_general(left, right, dims, preferred_element_type=F32)


def column_of(row):
    return jnp.broadcast_to(row, (128, row.shape[1])).T[:, :1]


def row_of(column):
    return jnp.broadcast_to(column, (column.shape[0], 128)).T[:1, :]


def equal_mask(left, right):
    return jnp.where(left == right, 1.0, 0.0).astype(BF16)


def iota(shape, dim):
    return lax.broadcasted_iota(jnp.int32, shape, dim).astype(F32)


class Links:
    def __init__(self, peers, grp):
        self.peers, self.grp = peers, grp
        self.me = lax.axis_index("dom") * grp + lax.axis_index("grp")

    def device(self, peer):
        return {"dom": peer // self.grp, "grp": lax.rem(peer, self.grp)}

    def other(self, step):
        return lax.rem(self.me + step, self.peers)

    def each(self, body):
        def step(i, carry):
            body(self.other(i))
            return carry

        lax.fori_loop(1, self.peers, step, 0)

    def greet(self):
        barrier = pltpu.get_barrier_semaphore()
        self.each(lambda peer: pl.semaphore_signal(
            barrier, inc=1, device_id=self.device(peer), device_id_type=pl.DeviceIdType.MESH))

    def greeted(self):
        pl.semaphore_wait(pltpu.get_barrier_semaphore(), self.peers - 1)

    def copy(self, src, dst, send, recv, peer, slot):
        return pltpu.make_async_remote_copy(
            src_ref=src, dst_ref=dst, send_sem=send.at[peer], recv_sem=recv.at[slot],
            device_id=self.device(peer), device_id_type=pl.DeviceIdType.MESH)

    def start(self, moves):
        def one(peer):
            for pick, dst, send, recv in moves:
                self.copy(pick(peer), dst.at[self.me], send, recv, peer, self.me).start()

        self.each(one)

    def finish(self, moves):
        def one(peer):
            for pick, dst, send, recv in moves:
                copy = self.copy(pick(peer), dst.at[peer], send, recv, peer, peer)
                copy.wait_recv()
                copy.wait_send()

        self.each(one)


def block_of(ref):
    return lambda peer: ref.at[peer]


def whole_of(ref):
    return lambda peer: ref


def sems(peers, count):
    return [pltpu.SemaphoreType.DMA((peers,)) for _ in range(2 * count)]


def call(body, outs, args, scratch=(), collective_id=None, smem=()):
    params = dict(vmem_limit_bytes=VMEM_LIMIT)
    if collective_id is not None:
        params.update(collective_id=collective_id, has_side_effects=True)
    return pl.pallas_call(
        body,
        out_shape=tuple(jax.ShapeDtypeStruct(s, d) for s, d in outs),
        in_specs=[
            pl.BlockSpec(memory_space=pltpu.SMEM if i in smem else pltpu.VMEM)
            for i in range(len(args))
        ],
        out_specs=tuple(pl.BlockSpec(memory_space=pltpu.VMEM) for _ in outs),
        scratch_shapes=list(scratch),
        compiler_params=pltpu.CompilerParams(**params),
    )(*args)


def first_exchange(peers, grp, feat, halo_row, request, wanted, arrived, outgoing, s0, r0, s1, r1):
    links = Links(peers, grp)
    links.greet()
    halo_len, width = outgoing.shape[1:]
    nodes = feat.shape[0]
    index = column_of(halo_row[...].astype(F32))
    pick = equal_mask(index, iota((index.shape[0], nodes), 1))
    outgoing[...] = dot(pick, feat[...]).astype(BF16).reshape(outgoing.shape)
    links.greeted()
    moves = [(block_of(request), wanted, s0, r0), (block_of(outgoing), arrived, s1, r1)]
    links.start(moves)
    wanted[links.me] = request[links.me]
    arrived[links.me] = outgoing[links.me]
    links.finish(moves)


def swap_blocks(peers, grp, sent, got, s0, r0):
    links = Links(peers, grp)
    links.greet()
    links.greeted()
    moves = [(block_of(sent), got, s0, r0)]
    links.start(moves)
    got[links.me] = sent[links.me]
    links.finish(moves)


def swap_grads(peers, grp, rows, terms, small, got, got_terms, got_small, s0, r0, s1, r1, s2, r2):
    links = Links(peers, grp)
    links.greet()
    links.greeted()
    moves = [
        (block_of(rows), got, s0, r0),
        (block_of(terms), got_terms, s1, r1),
        (whole_of(small), got_small, s2, r2),
    ]
    links.start(moves)
    got[links.me] = rows[links.me]
    got_terms[links.me] = terms[links.me]
    got_small[links.me] = small[...]
    links.finish(moves)


def last_exchange(
    peers, grp, halo, terms_s, terms_n, in_hidden,
    got, all_s, all_n, all_h, in_s, in_n, own_s, own_n, own_h,
    s0, r0, s1, r1, s2, r2, s3, r3, s4, r4, s5, r5,
):
    links = Links(peers, grp)
    me = links.me
    links.greet()
    own_h[...] = jnp.sum(in_hidden[...].astype(F32), axis=0).astype(BF16)
    links.greeted()
    terms = [(block_of(terms_s), in_s, s1, r1), (block_of(terms_n), in_n, s2, r2)]
    late = [(block_of(halo), got, s0, r0), (whole_of(own_h), all_h, s5, r5)]
    links.start(terms)
    links.start(late)
    in_s[me] = terms_s[me]
    in_n[me] = terms_n[me]
    got[me] = halo[me]
    all_h[me] = own_h[...]
    links.finish(terms)
    own_s[...] = jnp.sum(in_s[...].astype(F32), axis=0).astype(BF16)
    own_n[...] = jnp.sum(in_n[...].astype(F32), axis=0).astype(BF16)
    sums = [(whole_of(own_s), all_s, s3, r3), (whole_of(own_n), all_n, s4, r4)]
    links.start(sums)
    all_s[me] = own_s[...]
    all_n[me] = own_n[...]
    links.finish(late)
    links.finish(sums)


def wanted_column(wanted, req_len):
    peers = wanted.shape[0]
    spread = jnp.broadcast_to(wanted[...].astype(F32), (peers, req_len, 128)).reshape(peers * req_len, 128)
    lane = lax.broadcasted_iota(jnp.int32, spread.shape, 1)
    row = lax.rem(lax.broadcasted_iota(jnp.int32, spread.shape, 0), req_len)
    return jnp.sum(jnp.where(lane == row, spread, 0.0), axis=1, keepdims=True)


def count_edges(req_len, chunk, block, src, dst, count, wanted, counts, total, marks, ladder):
    rows, table_rows = counts.shape
    slots = src.shape[1]
    total[...] = jnp.zeros_like(total)
    index = wanted_column(wanted, req_len)
    ladder[...] = iota(ladder.shape, 0).astype(BF16)

    @pl.loop(0, slots // chunk)
    def _(c):
        span = pl.ds(pl.multiple_of(c * chunk, chunk), chunk)
        place = lax.broadcasted_iota(jnp.int32, (1, chunk), 1) + c * chunk
        into = jnp.where(place < count[0], dst[:, span], -1).astype(F32)
        marks[...] = equal_mask(index, into)
        source = src[:, span]
        high = source // block
        low = lax.rem(source, block)

        @pl.loop(0, table_rows // block)
        def _(b):
            here = jnp.where(high == b, low, -1).astype(F32).astype(BF16)
            hit = jnp.where(ladder[...] == here, jnp.array(1, BF16), jnp.array(0, BF16))
            cols = pl.ds(pl.multiple_of(b * block, block), block)
            total[:, cols] += dot(marks[...], hit, NT)

    counts[...] = total[...].astype(BF16)


def encode(req_len, block, feat, arrived, counts, wanted, w_self, w_neigh, served, feat_w, agg_w, floor):
    nodes, width = feat.shape
    rows, table_rows = counts.shape
    peers, halo_len = arrived.shape[:2]
    index = wanted_column(wanted, req_len)
    degree = jnp.sum(counts[...].astype(F32), axis=1, keepdims=True)
    floor_deg = jnp.maximum(degree, 1.0)
    sums = dot(counts[:, :nodes], feat[...])
    sums += dot(counts[:, nodes:], arrived[...].reshape(peers * halo_len, width))
    agg = (sums / floor_deg).astype(BF16)
    pick = equal_mask(index, iota((rows, nodes), 1))
    own = dot(pick, feat[...]).astype(BF16)
    emb = (dot(own, w_self[...]) + dot(agg, w_neigh[...])).astype(BF16)
    served[...] = emb.reshape(served.shape)
    feat_w[...] = own
    agg_w[...] = agg
    floor[...] = jnp.broadcast_to(floor_deg, floor.shape)


def encode_back(
    req_len, block, back, wanted, counts, feat_w, agg_w, floor, w_self, w_neigh,
    local, returned, grad_self, grad_neigh, near, far,
):
    nodes, width = local.shape
    rows, table_rows = counts.shape
    index = wanted_column(wanted, req_len)
    other = row_of(index)
    same = index == other
    earlier = lax.broadcasted_iota(jnp.int32, (rows, rows), 1) < lax.broadcasted_iota(jnp.int32, (rows, rows), 0)
    seen = jnp.sum(jnp.where(same & earlier, 1.0, 0.0), axis=1, keepdims=True)
    grad = dot(jnp.where(same, 1.0, 0.0).astype(BF16), back[...].reshape(rows, width))
    grad = jnp.where(seen > 0.0, 0.0, grad).astype(BF16)
    grad_self[...] = dot(feat_w[...], grad, TN).astype(BF16).reshape(grad_self.shape)
    grad_neigh[...] = dot(agg_w[...], grad, TN).astype(BF16).reshape(grad_neigh.shape)
    near[...] = dot(grad, w_self[...], NT).astype(BF16)
    far[...] = (dot(grad, w_neigh[...], NT) / floor[:, :1]).astype(BF16)

    @pl.loop(0, nodes // block)
    def _(b):
        cols = pl.ds(pl.multiple_of(b * block, block), block)
        spot = lax.broadcasted_iota(jnp.int32, (1, block), 1) + b * block
        pick = equal_mask(index, spot.astype(F32))
        local[cols, :] = dot(counts[:, cols], far[...], TN) + dot(pick, near[...], TN)

    halo = dot(counts[:, nodes:], far[...], TN)
    returned[...] = halo.astype(BF16).reshape(returned.shape)


def decode(
    chunk, received, ends, labels, weight, w_hidden, bias, w_out,
    logits, back, grad_hidden, small, picks, left_right, sums,
):
    peers, req_len, width = received.shape
    rows = peers * req_len
    got = received[...].reshape(rows, width)
    for place, half in ((0, w_hidden[:width, :]), (rows, w_hidden[width:, :])):
        exact = dot(got, half).T
        upper = exact.astype(BF16)
        left_right[0, :, place : place + rows] = upper
        left_right[1, :, place : place + rows] = (exact - upper.astype(F32)).astype(BF16)
    bias_col = column_of(bias[...])
    out_col = column_of(w_out[...])
    sums[...] = jnp.zeros_like(sums)
    slots = iota((rows, chunk), 0)

    def step(c, carry):
        bias_sum, out_sum = carry
        span = pl.ds(pl.multiple_of(c * chunk, chunk), chunk)
        end = ends[:, span].astype(F32)
        picks[:rows, :] = equal_mask(slots, end[:1, :])
        picks[rows:, :] = equal_mask(slots, end[1:, :])
        pre = dot(left_right[0], picks[...]) + dot(left_right[1], picks[...]) + bias_col
        hidden = jnp.maximum(pre, 0.0)
        logit = jnp.sum(hidden * out_col, axis=0, keepdims=True)
        logits[:, span] = logit
        slope = weight[:, span] * (jax.nn.sigmoid(logit) - labels[:, span].astype(F32))
        delta = jnp.where(pre > 0, slope * out_col, 0.0)
        sums[...] += dot(picks[...], delta.astype(BF16), NT)
        return (
            bias_sum + jnp.sum(delta, axis=1, keepdims=True),
            out_sum + jnp.sum(hidden * slope, axis=1, keepdims=True),
        )

    zero = jnp.zeros((width, 1), F32)
    bias_sum, out_sum = lax.fori_loop(0, ends.shape[1] // chunk, step, (zero, zero))
    small[0:1, :] = row_of(bias_sum)
    small[1:2, :] = row_of(out_sum)
    left = sums[:rows, :].astype(BF16)
    right = sums[rows:, :].astype(BF16)
    half = grad_hidden.shape[0] // 2
    shape = (half,) + grad_hidden.shape[1:]
    grad_hidden[:half] = dot(got, left, TN).astype(BF16).reshape(shape)
    grad_hidden[half:] = dot(got, right, TN).astype(BF16).reshape(shape)
    back_rows = dot(left, w_hidden[:width, :], NT) + dot(right, w_hidden[width:, :], NT)
    back[...] = back_rows.astype(BF16).reshape(back.shape)


def finish(local, halo_back, halo_row, in_s, in_n, in_h, in_small, out, g_s, g_n, g_h, g_b, g_o):
    nodes, width = local.shape
    rows = halo_row.shape[1]
    pick = equal_mask(iota((nodes, rows), 0), halo_row[...].astype(F32))
    out[...] = local[...] + dot(pick, halo_back[...].reshape(rows, width))
    g_s[...] = in_s[...].astype(F32).reshape(g_s.shape)
    g_n[...] = in_n[...].astype(F32).reshape(g_n.shape)
    g_h[...] = in_h[...].astype(F32).reshape(g_h.shape)
    small = jnp.sum(in_small[...], axis=0)
    g_b[...] = small[0:1, :]
    g_o[...] = small[1:2, :]


def per_device(
    features, edge_src, edge_dst, edge_count, halo_index, request_rows, pair_ends,
    labels, pair_weight, w_self, w_neigh, w_hidden, b_hidden, w_out,
):
    nodes, width = features.shape
    grp = lax.axis_size("grp")
    peers = lax.axis_size("dom") * grp
    halo_len = halo_index.shape[2]
    req_len = request_rows.shape[2]
    slots = edge_src.shape[0]
    pairs = labels.shape[0]
    table_rows = nodes + peers * halo_len
    rows = peers * req_len
    block = 256
    part = width // peers
    hidden_part = 2 * width // peers

    halo_row = halo_index.reshape(1, peers * halo_len)
    request = jnp.pad(request_rows[0], ((0, 0), (0, 128 - req_len))).reshape(peers, 1, 128)
    wanted, arrived = call(
        functools.partial(first_exchange, peers, grp),
        [((peers, 1, 128), jnp.int32), ((peers, halo_len, width), BF16)],
        (features, halo_row, request),
        [pltpu.VMEM((peers, halo_len, width), BF16)] + sems(peers, 2),
        collective_id=0,
    )
    edge_chunk = 2048
    (counts,) = call(
        functools.partial(count_edges, req_len, edge_chunk, block),
        [((rows, table_rows), BF16)],
        (edge_src.reshape(1, slots), edge_dst.reshape(1, slots), edge_count, wanted),
        [
            pltpu.VMEM((rows, table_rows), F32),
            pltpu.VMEM((rows, edge_chunk), BF16),
            pltpu.VMEM((block, edge_chunk), BF16),
        ],
        smem=(2,),
    )
    served, feat_w, agg_w, floor = call(
        functools.partial(encode, req_len, block),
        [
            ((peers, req_len, width), BF16),
            ((rows, width), BF16),
            ((rows, width), BF16),
            ((rows, 128), F32),
        ],
        (features, arrived, counts, wanted, w_self, w_neigh),
    )
    (received,) = call(
        functools.partial(swap_blocks, peers, grp),
        [((peers, req_len, width), BF16)],
        (served,),
        sems(peers, 1),
        collective_id=1,
    )
    pair_chunk = 512
    logits, back_sent, hidden_terms, small = call(
        functools.partial(decode, pair_chunk),
        [
            ((1, pairs), F32),
            ((peers, req_len, width), BF16),
            ((peers, hidden_part, width), BF16),
            ((2, width), F32),
        ],
        (
            received, pair_ends.T, labels.reshape(1, pairs), pair_weight.reshape(1, pairs),
            w_hidden, b_hidden.reshape(1, width), w_out.reshape(1, width),
        ),
        [
            pltpu.VMEM((2 * rows, pair_chunk), BF16),
            pltpu.VMEM((2, width, 2 * rows), BF16),
            pltpu.VMEM((2 * rows, width), F32),
        ],
    )
    back, in_hidden, in_small = call(
        functools.partial(swap_grads, peers, grp),
        [
            ((peers, req_len, width), BF16),
            ((peers, hidden_part, width), BF16),
            ((peers, 2, width), F32),
        ],
        (back_sent, hidden_terms, small),
        sems(peers, 3),
        collective_id=2,
    )
    local, returned, terms_s, terms_n = call(
        functools.partial(encode_back, req_len, block),
        [
            ((nodes, width), F32),
            ((peers, halo_len, width), BF16),
            ((peers, part, width), BF16),
            ((peers, part, width), BF16),
        ],
        (back, wanted, counts, feat_w, agg_w, floor, w_self, w_neigh),
        [pltpu.VMEM((rows, width), BF16), pltpu.VMEM((rows, width), BF16)],
    )
    halo_back, all_s, all_n, all_h = call(
        functools.partial(last_exchange, peers, grp),
        [
            ((peers, halo_len, width), BF16),
            ((peers, part, width), BF16),
            ((peers, part, width), BF16),
            ((peers, hidden_part, width), BF16),
        ],
        (returned, terms_s, terms_n, in_hidden),
        [
            pltpu.VMEM((peers, part, width), BF16),
            pltpu.VMEM((peers, part, width), BF16),
            pltpu.VMEM((part, width), BF16),
            pltpu.VMEM((part, width), BF16),
            pltpu.VMEM((hidden_part, width), BF16),
        ] + sems(peers, 6),
        collective_id=3,
    )
    grad_features, g_s, g_n, g_h, g_b, g_o = call(
        finish,
        [
            ((nodes, width), F32),
            ((width, width), F32),
            ((width, width), F32),
            ((2 * width, width), F32),
            ((1, width), F32),
            ((1, width), F32),
        ],
        (local, halo_back, halo_row, all_s, all_n, all_h, in_small),
    )
    return (logits.reshape(pairs), grad_features, g_s, g_n, g_h, g_b.reshape(width), g_o.reshape(width))


def solution(mesh):
    both = ("dom", "grp")
    in_specs = (
        P(both, None), P(both), P(both), P(both), P(both, None, None), P(both, None, None),
        P(both, None), P(both), P(both), P(), P(), P(), P(), P(),
    )
    out_specs = (P(both), P(both, None), P(), P(), P(), P(), P())
    return jax.shard_map(
        per_device, mesh=mesh, in_specs=in_specs, out_specs=out_specs, check_vma=False
    )
```

```python
import functools

import jax
import jax.numpy as jnp
from jax import lax
from jax.experimental import pallas as pl
from jax.experimental.pallas import tpu as pltpu
from jax.sharding import PartitionSpec as P

F32 = jnp.float32
BF16 = jnp.bfloat16
F8 = jnp.float8_e4m3fn
VMEM_LIMIT = 60 * 1024 * 1024
NN = (((1,), (0,)), ((), ()))
NT = (((1,), (1,)), ((), ()))
TN = (((0,), (0,)), ((), ()))


def dot(left, right, dims=NN):
    return lax.dot_general(left, right, dims, preferred_element_type=F32)


def column_of(row):
    return jnp.broadcast_to(row, (128, row.shape[1])).T[:, :1]


def row_of(column):
    return jnp.broadcast_to(column, (column.shape[0], 128)).T[:1, :]


def equal_mask(left, right):
    return jnp.where(left == right, 1.0, 0.0).astype(BF16)


def iota(shape, dim):
    return lax.broadcasted_iota(jnp.int32, shape, dim).astype(F32)


class Links:
    def __init__(self, peers, grp):
        self.peers, self.grp = peers, grp
        self.me = lax.axis_index("dom") * grp + lax.axis_index("grp")

    def device(self, peer):
        return {"dom": peer // self.grp, "grp": lax.rem(peer, self.grp)}

    def other(self, step):
        return lax.rem(self.me + step, self.peers)

    def each(self, body):
        def step(i, carry):
            body(self.other(i))
            return carry

        lax.fori_loop(1, self.peers, step, 0)

    def greet(self):
        barrier = pltpu.get_barrier_semaphore()
        self.each(lambda peer: pl.semaphore_signal(
            barrier, inc=1, device_id=self.device(peer), device_id_type=pl.DeviceIdType.MESH))

    def greeted(self):
        pl.semaphore_wait(pltpu.get_barrier_semaphore(), self.peers - 1)

    def copy(self, src, dst, send, recv, peer, slot):
        return pltpu.make_async_remote_copy(
            src_ref=src, dst_ref=dst, send_sem=send.at[peer], recv_sem=recv.at[slot],
            device_id=self.device(peer), device_id_type=pl.DeviceIdType.MESH)

    def start(self, moves):
        def one(peer):
            for pick, dst, send, recv in moves:
                self.copy(pick(peer), dst.at[self.me], send, recv, peer, self.me).start()

        self.each(one)

    def finish(self, moves):
        def one(peer):
            for pick, dst, send, recv in moves:
                copy = self.copy(pick(peer), dst.at[peer], send, recv, peer, peer)
                copy.wait_recv()
                copy.wait_send()

        self.each(one)


def block_of(ref):
    return lambda peer: ref.at[peer]


def whole_of(ref):
    return lambda peer: ref


def sems(peers, count):
    return [pltpu.SemaphoreType.DMA((peers,)) for _ in range(2 * count)]


def call(body, outs, args, scratch=(), collective_id=None, smem=()):
    params = dict(vmem_limit_bytes=VMEM_LIMIT)
    if collective_id is not None:
        params.update(collective_id=collective_id, has_side_effects=True)
    return pl.pallas_call(
        body,
        out_shape=tuple(jax.ShapeDtypeStruct(s, d) for s, d in outs),
        in_specs=[
            pl.BlockSpec(memory_space=pltpu.SMEM if i in smem else pltpu.VMEM)
            for i in range(len(args))
        ],
        out_specs=tuple(pl.BlockSpec(memory_space=pltpu.VMEM) for _ in outs),
        scratch_shapes=list(scratch),
        compiler_params=pltpu.CompilerParams(**params),
    )(*args)


def first_exchange(peers, grp, feat, halo_row, request, wanted, arrived, outgoing, s0, r0, s1, r1):
    links = Links(peers, grp)
    links.greet()
    halo_len, width = outgoing.shape[1:]
    nodes = feat.shape[0]
    index = column_of(halo_row[...].astype(F32))
    pick = equal_mask(index, iota((index.shape[0], nodes), 1))
    outgoing[...] = dot(pick, feat[...]).astype(BF16).reshape(outgoing.shape)
    links.greeted()
    moves = [(block_of(request), wanted, s0, r0), (block_of(outgoing), arrived, s1, r1)]
    links.start(moves)
    wanted[links.me] = request[links.me]
    arrived[links.me] = outgoing[links.me]
    links.finish(moves)


def swap_blocks(peers, grp, sent, got, s0, r0):
    links = Links(peers, grp)
    links.greet()
    links.greeted()
    moves = [(block_of(sent), got, s0, r0)]
    links.start(moves)
    got[links.me] = sent[links.me]
    links.finish(moves)


def swap_grads(peers, grp, rows, terms, small, got, got_terms, got_small, s0, r0, s1, r1, s2, r2):
    links = Links(peers, grp)
    links.greet()
    links.greeted()
    moves = [
        (block_of(rows), got, s0, r0),
        (block_of(terms), got_terms, s1, r1),
        (whole_of(small), got_small, s2, r2),
    ]
    links.start(moves)
    got[links.me] = rows[links.me]
    got_terms[links.me] = terms[links.me]
    got_small[links.me] = small[...]
    links.finish(moves)


def last_exchange(
    peers, grp, halo, terms_s, terms_n, in_hidden,
    got, all_s, all_n, all_h, in_s, in_n, own_s, own_n, own_h,
    s0, r0, s1, r1, s2, r2, s3, r3, s4, r4, s5, r5,
):
    links = Links(peers, grp)
    me = links.me
    links.greet()
    own_h[...] = jnp.sum(in_hidden[...].astype(F32), axis=0).astype(BF16)
    links.greeted()
    terms = [(block_of(terms_s), in_s, s1, r1), (block_of(terms_n), in_n, s2, r2)]
    late = [(block_of(halo), got, s0, r0), (whole_of(own_h), all_h, s5, r5)]
    links.start(terms)
    links.start(late)
    in_s[me] = terms_s[me]
    in_n[me] = terms_n[me]
    got[me] = halo[me]
    all_h[me] = own_h[...]
    links.finish(terms)
    own_s[...] = jnp.sum(in_s[...].astype(F32), axis=0).astype(BF16)
    own_n[...] = jnp.sum(in_n[...].astype(F32), axis=0).astype(BF16)
    sums = [(whole_of(own_s), all_s, s3, r3), (whole_of(own_n), all_n, s4, r4)]
    links.start(sums)
    all_s[me] = own_s[...]
    all_n[me] = own_n[...]
    links.finish(late)
    links.finish(sums)


def wanted_column(wanted, req_len):
    peers = wanted.shape[0]
    spread = jnp.broadcast_to(wanted[...].astype(F32), (peers, req_len, 128)).reshape(peers * req_len, 128)
    lane = lax.broadcasted_iota(jnp.int32, spread.shape, 1)
    row = lax.rem(lax.broadcasted_iota(jnp.int32, spread.shape, 0), req_len)
    return jnp.sum(jnp.where(lane == row, spread, 0.0), axis=1, keepdims=True)


def count_edges(req_len, chunk, block, src, dst, count, wanted, counts, total, marks, ladder):
    rows, table_rows = counts.shape
    slots = src.shape[1]
    total[...] = jnp.zeros_like(total)
    index = wanted_column(wanted, req_len)
    ladder[...] = iota(ladder.shape, 0).astype(BF16)

    @pl.loop(0, slots // chunk)
    def _(c):
        span = pl.ds(pl.multiple_of(c * chunk, chunk), chunk)
        place = lax.broadcasted_iota(jnp.int32, (1, chunk), 1) + c * chunk
        into = jnp.where(place < count[0], dst[:, span], -1).astype(F32)
        marks[...] = jnp.where(index == into, 1.0, 0.0).astype(F8)
        source = src[:, span]
        high = source // block
        low = lax.rem(source, block)

        @pl.loop(0, table_rows // block)
        def _(b):
            here = jnp.where(high == b, low, -1).astype(F32).astype(BF16)
            hit = jnp.where(ladder[...] == here, jnp.array(1, BF16), jnp.array(0, BF16)).astype(F8)
            cols = pl.ds(pl.multiple_of(b * block, block), block)
            total[:, cols] += dot(marks[...], hit, NT)

    counts[...] = total[...].astype(BF16)


def encode(req_len, block, feat, arrived, counts, wanted, w_self, w_neigh, served, feat_w, agg_w, floor):
    nodes, width = feat.shape
    rows, table_rows = counts.shape
    peers, halo_len = arrived.shape[:2]
    index = wanted_column(wanted, req_len)
    degree = jnp.sum(counts[...].astype(F32), axis=1, keepdims=True)
    floor_deg = jnp.maximum(degree, 1.0)
    sums = dot(counts[:, :nodes], feat[...])
    sums += dot(counts[:, nodes:], arrived[...].reshape(peers * halo_len, width))
    agg = (sums / floor_deg).astype(BF16)
    pick = equal_mask(index, iota((rows, nodes), 1))
    own = dot(pick, feat[...]).astype(BF16)
    emb = (dot(own, w_self[...]) + dot(agg, w_neigh[...])).astype(BF16)
    served[...] = emb.reshape(served.shape)
    feat_w[...] = own
    agg_w[...] = agg
    floor[...] = jnp.broadcast_to(floor_deg, floor.shape)


def encode_back(
    req_len, block, back, wanted, counts, feat_w, agg_w, floor, w_self, w_neigh,
    local, returned, grad_self, grad_neigh, near, far,
):
    nodes, width = local.shape
    rows, table_rows = counts.shape
    index = wanted_column(wanted, req_len)
    other = row_of(index)
    same = index == other
    earlier = lax.broadcasted_iota(jnp.int32, (rows, rows), 1) < lax.broadcasted_iota(jnp.int32, (rows, rows), 0)
    seen = jnp.sum(jnp.where(same & earlier, 1.0, 0.0), axis=1, keepdims=True)
    grad = dot(jnp.where(same, 1.0, 0.0).astype(BF16), back[...].reshape(rows, width))
    grad = jnp.where(seen > 0.0, 0.0, grad).astype(BF16)
    grad_self[...] = dot(feat_w[...], grad, TN).astype(BF16).reshape(grad_self.shape)
    grad_neigh[...] = dot(agg_w[...], grad, TN).astype(BF16).reshape(grad_neigh.shape)
    near[...] = dot(grad, w_self[...], NT).astype(BF16)
    far[...] = (dot(grad, w_neigh[...], NT) / floor[:, :1]).astype(BF16)

    @pl.loop(0, nodes // block)
    def _(b):
        cols = pl.ds(pl.multiple_of(b * block, block), block)
        spot = lax.broadcasted_iota(jnp.int32, (1, block), 1) + b * block
        pick = equal_mask(index, spot.astype(F32))
        local[cols, :] = dot(counts[:, cols], far[...], TN) + dot(pick, near[...], TN)

    halo = dot(counts[:, nodes:], far[...], TN)
    returned[...] = halo.astype(BF16).reshape(returned.shape)


def decode(
    chunk, received, ends, labels, weight, w_hidden, bias, w_out,
    logits, back, grad_hidden, small, picks, left_right, sums,
):
    peers, req_len, width = received.shape
    rows = peers * req_len
    got = received[...].reshape(rows, width)
    for place, half in ((0, w_hidden[:width, :]), (rows, w_hidden[width:, :])):
        exact = dot(got, half).T
        upper = exact.astype(BF16)
        left_right[0, :, place : place + rows] = upper
        left_right[1, :, place : place + rows] = (exact - upper.astype(F32)).astype(BF16)
    bias_col = column_of(bias[...])
    out_col = column_of(w_out[...])
    sums[...] = jnp.zeros_like(sums)
    slots = iota((rows, chunk), 0)

    def step(c, carry):
        bias_sum, out_sum = carry
        span = pl.ds(pl.multiple_of(c * chunk, chunk), chunk)
        end = ends[:, span].astype(F32)
        picks[:rows, :] = equal_mask(slots, end[:1, :])
        picks[rows:, :] = equal_mask(slots, end[1:, :])
        pre = dot(left_right[0], picks[...]) + dot(left_right[1], picks[...]) + bias_col
        hidden = jnp.maximum(pre, 0.0)
        logit = jnp.sum(hidden * out_col, axis=0, keepdims=True)
        logits[:, span] = logit
        slope = weight[:, span] * (jax.nn.sigmoid(logit) - labels[:, span].astype(F32))
        delta = jnp.where(pre > 0, slope * out_col, 0.0)
        sums[...] += dot(picks[...], delta.astype(BF16), NT)
        return (
            bias_sum + jnp.sum(delta, axis=1, keepdims=True),
            out_sum + jnp.sum(hidden * slope, axis=1, keepdims=True),
        )

    zero = jnp.zeros((width, 1), F32)
    bias_sum, out_sum = lax.fori_loop(0, ends.shape[1] // chunk, step, (zero, zero))
    small[0:1, :] = row_of(bias_sum)
    small[1:2, :] = row_of(out_sum)
    left = sums[:rows, :].astype(BF16)
    right = sums[rows:, :].astype(BF16)
    half = grad_hidden.shape[0] // 2
    shape = (half,) + grad_hidden.shape[1:]
    grad_hidden[:half] = dot(got, left, TN).astype(BF16).reshape(shape)
    grad_hidden[half:] = dot(got, right, TN).astype(BF16).reshape(shape)
    back_rows = dot(left, w_hidden[:width, :], NT) + dot(right, w_hidden[width:, :], NT)
    back[...] = back_rows.astype(BF16).reshape(back.shape)


def finish(local, halo_back, halo_row, in_s, in_n, in_h, in_small, out, g_s, g_n, g_h, g_b, g_o):
    nodes, width = local.shape
    rows = halo_row.shape[1]
    pick = equal_mask(iota((nodes, rows), 0), halo_row[...].astype(F32))
    out[...] = local[...] + dot(pick, halo_back[...].reshape(rows, width))
    g_s[...] = in_s[...].astype(F32).reshape(g_s.shape)
    g_n[...] = in_n[...].astype(F32).reshape(g_n.shape)
    g_h[...] = in_h[...].astype(F32).reshape(g_h.shape)
    small = jnp.sum(in_small[...], axis=0)
    g_b[...] = small[0:1, :]
    g_o[...] = small[1:2, :]


def per_device(
    features, edge_src, edge_dst, edge_count, halo_index, request_rows, pair_ends,
    labels, pair_weight, w_self, w_neigh, w_hidden, b_hidden, w_out,
):
    nodes, width = features.shape
    grp = lax.axis_size("grp")
    peers = lax.axis_size("dom") * grp
    halo_len = halo_index.shape[2]
    req_len = request_rows.shape[2]
    slots = edge_src.shape[0]
    pairs = labels.shape[0]
    table_rows = nodes + peers * halo_len
    rows = peers * req_len
    block = 256
    part = width // peers
    hidden_part = 2 * width // peers

    halo_row = halo_index.reshape(1, peers * halo_len)
    request = jnp.pad(request_rows[0], ((0, 0), (0, 128 - req_len))).reshape(peers, 1, 128)
    wanted, arrived = call(
        functools.partial(first_exchange, peers, grp),
        [((peers, 1, 128), jnp.int32), ((peers, halo_len, width), BF16)],
        (features, halo_row, request),
        [pltpu.VMEM((peers, halo_len, width), BF16)] + sems(peers, 2),
        collective_id=0,
    )
    edge_chunk = 2048
    (counts,) = call(
        functools.partial(count_edges, req_len, edge_chunk, block),
        [((rows, table_rows), BF16)],
        (edge_src.reshape(1, slots), edge_dst.reshape(1, slots), edge_count, wanted),
        [
            pltpu.VMEM((rows, table_rows), F32),
            pltpu.VMEM((rows, edge_chunk), F8),
            pltpu.VMEM((block, edge_chunk), BF16),
        ],
        smem=(2,),
    )
    served, feat_w, agg_w, floor = call(
        functools.partial(encode, req_len, block),
        [
            ((peers, req_len, width), BF16),
            ((rows, width), BF16),
            ((rows, width), BF16),
            ((rows, 128), F32),
        ],
        (features, arrived, counts, wanted, w_self, w_neigh),
    )
    (received,) = call(
        functools.partial(swap_blocks, peers, grp),
        [((peers, req_len, width), BF16)],
        (served,),
        sems(peers, 1),
        collective_id=1,
    )
    pair_chunk = 512
    logits, back_sent, hidden_terms, small = call(
        functools.partial(decode, pair_chunk),
        [
            ((1, pairs), F32),
            ((peers, req_len, width), BF16),
            ((peers, hidden_part, width), BF16),
            ((2, width), F32),
        ],
        (
            received, pair_ends.T, labels.reshape(1, pairs), pair_weight.reshape(1, pairs),
            w_hidden, b_hidden.reshape(1, width), w_out.reshape(1, width),
        ),
        [
            pltpu.VMEM((2 * rows, pair_chunk), BF16),
            pltpu.VMEM((2, width, 2 * rows), BF16),
            pltpu.VMEM((2 * rows, width), F32),
        ],
    )
    back, in_hidden, in_small = call(
        functools.partial(swap_grads, peers, grp),
        [
            ((peers, req_len, width), BF16),
            ((peers, hidden_part, width), BF16),
            ((peers, 2, width), F32),
        ],
        (back_sent, hidden_terms, small),
        sems(peers, 3),
        collective_id=2,
    )
    local, returned, terms_s, terms_n = call(
        functools.partial(encode_back, req_len, block),
        [
            ((nodes, width), F32),
            ((peers, halo_len, width), BF16),
            ((peers, part, width), BF16),
            ((peers, part, width), BF16),
        ],
        (back, wanted, counts, feat_w, agg_w, floor, w_self, w_neigh),
        [pltpu.VMEM((rows, width), BF16), pltpu.VMEM((rows, width), BF16)],
    )
    halo_back, all_s, all_n, all_h = call(
        functools.partial(last_exchange, peers, grp),
        [
            ((peers, halo_len, width), BF16),
            ((peers, part, width), BF16),
            ((peers, part, width), BF16),
            ((peers, hidden_part, width), BF16),
        ],
        (returned, terms_s, terms_n, in_hidden),
        [
            pltpu.VMEM((peers, part, width), BF16),
            pltpu.VMEM((peers, part, width), BF16),
            pltpu.VMEM((part, width), BF16),
            pltpu.VMEM((part, width), BF16),
            pltpu.VMEM((hidden_part, width), BF16),
        ] + sems(peers, 6),
        collective_id=3,
    )
    grad_features, g_s, g_n, g_h, g_b, g_o = call(
        finish,
        [
            ((nodes, width), F32),
            ((width, width), F32),
            ((width, width), F32),
            ((2 * width, width), F32),
            ((1, width), F32),
            ((1, width), F32),
        ],
        (local, halo_back, halo_row, all_s, all_n, all_h, in_small),
    )
    return (logits.reshape(pairs), grad_features, g_s, g_n, g_h, g_b.reshape(width), g_o.reshape(width))


def solution(mesh):
    both = ("dom", "grp")
    in_specs = (
        P(both, None), P(both), P(both), P(both), P(both, None, None), P(both, None, None),
        P(both, None), P(both), P(both), P(), P(), P(), P(), P(),
    )
    out_specs = (P(both), P(both, None), P(), P(), P(), P(), P())
    return jax.shard_map(
        per_device, mesh=mesh, in_specs=in_specs, out_specs=out_specs, check_vma=False
    )
```
